32 devices in a mesh: blk: 8 (over z, core), col: 4 (over y, x).
Axes of the slice: x: 2, y: 2, z: 4, core: 2. Of those that a mesh axis runs over, the one named last changes fastest.
Arguments:
- source_coords: bfloat16 [96, 8192], P(None, 'blk'), may hold values from -0.61 to 0.61
- target_coords: bfloat16 [96, 4096], P(None, ('blk', 'col')), may hold values from -0.61 to 0.61
- source_mass: float32 [8192], P('blk'), may hold values from 1.2207031e-05 to 0.0012207031
- target_mass: float32 [4096], P(('blk', 'col')), may hold values from 2.4414063e-05 to 0.0024414062
Outputs:
- source_potential: float32 [8192], P('blk')
- target_potential: float32 [4096], P(('blk', 'col'))
- dual_bound: float32 [], replicated
The draws below stay inside these ranges and needn't reach their ends.
All inputs are finite; a program needn't handle non-finite values.
Results may differ from the reference program's by a relative error of at most 0.0003.
Values sent between devices are 32-bit elements; how exact they have to be, the bound alone decides.
A program may use at most 64 MiB of HBM per device.

```python
import math
import jax
import jax.numpy as jnp
from jax import lax

FEAT = 96
ROUNDS = 2
N_SRC = 8192
N_TGT = 4096


def point_cloud(key, salt, columns, heading):
    first_key = jax.random.fold_in(jax.random.fold_in(key, salt), 0)
    third_key = jax.random.fold_in(jax.random.fold_in(key, salt), 2)
    fourth_key = jax.random.fold_in(jax.random.fold_in(key, salt), 3)
    values = jnp.clip(0.1 * jax.random.normal(first_key, (FEAT, columns), jnp.float32), -0.6, 0.6)
    offset = jax.random.randint(third_key, (), 0, 16)
    position = jnp.arange(columns)
    distant = (position + offset) % 16 == 0
    level = jax.random.randint(fourth_key, (columns,), 0, 3).astype(jnp.float32)
    strength = 0.2 + 0.15 * level
    signs = jnp.where(jax.random.uniform(jax.random.fold_in(key, 77), (FEAT, 1), jnp.float32) < 0.5, -1.0, 1.0)
    moved = heading * signs * strength[None, :] + jnp.clip(values, -0.11, 0.11)
    values = jnp.where(distant[None, :], moved, values)
    return values.astype(jnp.bfloat16)


def draw_source_coords(key, part):
    return point_cloud(key, 11, N_SRC, 1.0)


def draw_target_coords(key, part):
    return point_cloud(key, 23, N_TGT, -1.0)


def levels(stream_key, extent, cuts, least, high):
    def one(dim, shards_of):
        draws = jax.random.uniform(jax.random.fold_in(jax.random.fold_in(stream_key, 6), dim), (shards_of,), jnp.float32, least / len(cuts), high / len(cuts))
        return jnp.repeat(jnp.exp(draws), extent[dim] // shards_of).reshape((-1,) + (1,) * (len(extent) - dim - 1))

    gain = one(*cuts[0])
    for cut in cuts[1:]:
        gain = gain * one(*cut)
    return gain


def setup_inputs(seed: int = 0) -> dict:
    splits = jax.random.split(jax.random.key(seed), 5)
    source_coords = draw_source_coords(jax.random.fold_in(splits[4], 71), 0)
    target_coords = draw_target_coords(jax.random.fold_in(splits[4], 71), 0)
    source_mass = jnp.clip(jnp.exp(math.log(0.0012207031) - 4.6051702 * jax.random.uniform(splits[2], (N_SRC,), jnp.float32) ** levels(splits[2], (N_SRC,), ((0, 8),), -0.2, 0.2)), 1.220703143189894e-05, 0.0012207031)
    target_mass = jnp.clip(jnp.exp(math.log(0.0024414062) - 4.6051702 * jax.random.uniform(splits[3], (N_TGT,), jnp.float32) ** levels(splits[3], (N_TGT,), ((0, 32),), -0.2, 0.2)), 2.441406286379788e-05, 0.0024414062)
    return {"source_coords": source_coords, "target_coords": target_coords, "source_mass": source_mass, "target_mass": target_mass}


EPSILON = 0.05
tile_width = 2048


def inner_products(left_coords, right_coords):
    return lax.dot_general(left_coords, right_coords, (((0,), (0,)), ((), ())), preferred_element_type=jnp.float32)


def split_tiles(values, tile_cols):
    number = values.shape[-1] // tile_cols
    return jnp.moveaxis(values.reshape(values.shape[:-1] + (number, tile_cols)), -2, 0)


def reduce_axis(scores, along):
    maxima = jnp.max(scores, axis=along)
    totals = jnp.sum(jnp.exp(scores - jnp.expand_dims(maxima, along)), axis=along)
    return maxima, totals


def merge_lse(first, second):
    first_max, first_sum = first
    second_max, second_sum = second
    maxima = jnp.maximum(first_max, second_max)
    return maxima, first_sum * jnp.exp(first_max - maxima) + second_sum * jnp.exp(second_max - maxima)


def reference(source_coords, target_coords, source_mass, target_mass):
    source_count = source_coords.shape[1]
    target_count = target_coords.shape[1]
    source_sq = jnp.sum(jnp.square(source_coords.astype(jnp.float32)), axis=0)
    target_sq = jnp.sum(jnp.square(target_coords.astype(jnp.float32)), axis=0)
    source_logs = jnp.log(source_mass)
    target_logs = jnp.log(target_mass)
    tile_cols = math.gcd(target_count, tile_width)
    coord_tiles = split_tiles(target_coords, tile_cols)
    square_tiles = split_tiles(target_sq, tile_cols)
    log_tiles = split_tiles(target_logs, tile_cols)

    def cost_tile(tile_coords, tile_sq):
        return (source_sq[:, None] + tile_sq[None, :]) - 2.0 * inner_products(source_coords, tile_coords)

    def row_update(col_dual):
        dual_tiles = split_tiles(col_dual, tile_cols)

        def advance(running, element):
            tile_coords, tile_sq, tile_logs, tile_dual = element
            scores = tile_logs[None, :] + (tile_dual[None, :] - cost_tile(tile_coords, tile_sq)) / EPSILON
            return merge_lse(running, reduce_axis(scores, 1)), None

        blank_rows = (jnp.full((source_count,), -jnp.inf, jnp.float32), jnp.zeros((source_count,), jnp.float32))
        (maxima, totals), _ = lax.scan(advance, blank_rows, (coord_tiles, square_tiles, log_tiles, dual_tiles))
        return -EPSILON * (maxima + jnp.log(totals))

    def col_update(row_dual):
        def column_tile(element):
            tile_coords, tile_sq = element
            scores = source_logs[:, None] + (row_dual[:, None] - cost_tile(tile_coords, tile_sq)) / EPSILON
            maxima, totals = reduce_axis(scores, 0)
            return -EPSILON * (maxima + jnp.log(totals))

        return lax.map(column_tile, (coord_tiles, square_tiles)).reshape(target_count)

    col_dual = jnp.zeros((target_count,), jnp.float32)
    for round_index in range(ROUNDS):
        row_dual = row_update(col_dual)
        col_dual = col_update(row_dual)

    dual_tiles = split_tiles(col_dual, tile_cols)

    def lower(running, element):
        tile_coords, tile_sq, tile_dual = element
        values = cost_tile(tile_coords, tile_sq) - tile_dual[None, :]
        return jnp.minimum(running, jnp.min(values, axis=1)), None

    source_potential, _ = lax.scan(lower, jnp.full((source_count,), jnp.inf, jnp.float32), (coord_tiles, square_tiles, dual_tiles))
    dual_bound = jnp.sum(source_mass * source_potential) + jnp.sum(target_mass * col_dual)
    return source_potential, col_dual, dual_bound
```

```python
import functools

import jax
import jax.numpy as jnp
from jax import lax
from jax.experimental import pallas as pl
from jax.experimental.pallas import tpu as pltpu
from jax.sharding import PartitionSpec as P

ROUNDS = 2
EPSILON = 0.05
LANES = 128
EXTRA = 8
F32 = jnp.float32
BF16 = jnp.bfloat16
SCALE = 1.4426950408889634 / EPSILON
MESH = pl.DeviceIdType.MESH


def soft(total):
    return EPSILON * jnp.log(total)


def row_tile(reds, wide):
    position = lax.broadcasted_iota(jnp.int32, (8, LANES), 0)
    out = jnp.zeros((8, LANES), F32)
    for index, part in enumerate(reds):
        out = jnp.where(position == index, jnp.broadcast_to(part, (8, LANES)), out)
    return out


def three_parts(value):
    high = value.astype(BF16).astype(F32)
    rest = value - high
    middle = rest.astype(BF16).astype(F32)
    return high, middle, rest - middle


def set_bias(left_ref, value, feats_pad):
    parts = three_parts(value)
    for r in range(value.shape[0]):
        tile = row_tile([part[r : r + 1, :] for part in parts], LANES)
        left_ref[r * LANES : (r + 1) * LANES, feats_pad : feats_pad + 8] = tile.T.astype(BF16)


def reduce_pass(left_ref, right_ref, out_ref, slot, hard, chunk):
    number = right_ref.shape[1] // chunk

    def body(c, carry):
        lanes = pl.ds(pl.multiple_of(c * chunk, chunk), chunk)
        scores = jnp.dot(left_ref[...], right_ref[:, lanes], preferred_element_type=F32)
        value = jnp.max(scores, axis=0, keepdims=True)
        if not hard:
            total = jnp.sum(jnp.exp2((scores - value) * SCALE), axis=0, keepdims=True)
            value = value + soft(total)
        for r in range(chunk // LANES):
            out_ref[slot, pl.ds(c * (chunk // LANES) + r, 1), :] = value[
                :, r * LANES : (r + 1) * LANES
            ]
        return carry

    lax.fori_loop(0, number, body, 0)


def copies(axis, extent, buf, send, recv):
    me = lax.axis_index(axis)
    started = []
    for k in range(1, extent):
        started.append(
            pltpu.make_async_remote_copy(
                src_ref=buf.at[me],
                dst_ref=buf.at[me],
                send_sem=send.at[k - 1],
                recv_sem=recv.at[k - 1],
                device_id={axis: lax.rem(me + k, extent)},
                device_id_type=MESH,
            )
        )
    return started


def arrival(axis, extent, buf, send, recv, k):
    me = lax.axis_index(axis)
    origin = lax.rem(me + extent - k, extent)
    return pltpu.make_async_remote_copy(
        src_ref=buf.at[origin],
        dst_ref=buf.at[origin],
        send_sem=send.at[k - 1],
        recv_sem=recv.at[k - 1],
        device_id={axis: origin},
        device_id_type=MESH,
    )


def exchange(axis, extent, buf, send, recv):
    started = copies(axis, extent, buf, send, recv)
    for copy in started:
        copy.start()
    for k in range(1, extent):
        arrival(axis, extent, buf, send, recv, k).wait_recv()
    return started


def merge(parts):
    top = jnp.max(parts, axis=0)
    return top + soft(jnp.sum(jnp.exp2((parts - top[None]) * SCALE), axis=0))


def kernel(
    nb, nc, feats, feats_pad,
    sc_ref, tc_ref, sm_ref, tm_ref,
    sp_ref, tp_ref, db_ref,
    blocks, a_right, a_left, b_right, b_left, rows, cols, lows, sums,
    g_send, g_recv, r_send, r_recv, c_send, c_recv, m_send, m_recv, d_send, d_recv,
):
    bi = lax.axis_index("blk")
    ci = lax.axis_index("col")
    ns = sc_ref.shape[1]
    ts = tc_ref.shape[1]
    gs = ns // LANES
    gt = ts // LANES
    barrier = pltpu.get_barrier_semaphore()
    for k in range(1, nb):
        pl.semaphore_signal(barrier, inc=1, device_id={"blk": lax.rem(bi + k, nb)}, device_id_type=MESH)
    for k in range(1, nc):
        pl.semaphore_signal(barrier, inc=1, device_id={"col": lax.rem(ci + k, nc)}, device_id_type=MESH)

    own = tc_ref[...].astype(F32)
    blocks[bi, 0:feats, :] = own
    for g in range(gt):
        lanes = slice(g * LANES, (g + 1) * LANES)
        blocks[bi, feats : feats + EXTRA, lanes] = row_tile(
            [tm_ref[g : g + 1, :], jnp.sum(jnp.square(own[:, lanes]), axis=0, keepdims=True)], LANES
        )

    depth = a_right.shape[0]
    ones = lambda width: jnp.where(
        lax.broadcasted_iota(jnp.int32, (depth - feats_pad, width), 0) < 3, 1.0, 0.0
    ).astype(BF16)

    pl.semaphore_wait(barrier, nb + nc - 2)
    gathers = copies("blk", nb, blocks, g_send, g_recv)
    for copy in gathers:
        copy.start()

    a_right[0:feats, :] = sc_ref[...]
    if feats_pad > feats:
        a_right[feats:feats_pad, :] = jnp.zeros((feats_pad - feats, ns), BF16)
        b_right[feats:feats_pad, :] = jnp.zeros((feats_pad - feats, b_right.shape[1]), BF16)
    a_right[feats_pad:depth, :] = ones(ns)
    b_right[feats_pad:depth, :] = ones(b_right.shape[1])
    wide = sc_ref[...].astype(F32)
    source_sq = jnp.sum(jnp.square(wide), axis=0, keepdims=True)
    for r in range(gs):
        rows_of = slice(r * LANES, (r + 1) * LANES)
        piece = jnp.concatenate(
            [wide[:, rows_of], jnp.zeros((feats_pad - feats, LANES), F32)], axis=0
        )
        a_left[rows_of, 0:feats_pad] = piece.T.astype(BF16)
    a_left[:, feats_pad:depth] = jnp.zeros((ns, depth - feats_pad), BF16)
    b_left[:, feats_pad:depth] = jnp.zeros((b_left.shape[0], depth - feats_pad), BF16)
    source_bias = EPSILON * jnp.log(sm_ref[...])

    for k in range(1, nb):
        arrival("blk", nb, blocks, g_send, g_recv, k).wait_recv()
    masses = []
    squares = []
    for b in range(nb):
        for g in range(gt):
            lanes = slice(g * LANES, (g + 1) * LANES)
            rows_of = slice(b * ts + g * LANES, b * ts + (g + 1) * LANES)
            piece = 2.0 * blocks[b, 0:feats, lanes]
            b_right[0:feats, rows_of] = piece.astype(BF16)
            if feats_pad > feats:
                piece = jnp.concatenate(
                    [piece, jnp.zeros((feats_pad - feats, LANES), F32)], axis=0
                )
            b_left[rows_of, 0:feats_pad] = piece.T.astype(BF16)
            masses.append(blocks[b, feats : feats + 1, lanes])
            squares.append(blocks[b, feats + 1 : feats + 2, lanes])
    target_mass = jnp.concatenate(masses, axis=0)
    target_sq = jnp.concatenate(squares, axis=0)
    target_bias = EPSILON * jnp.log(target_mass)

    chunk = 256
    pending = list(gathers)
    held = -target_sq
    for round_index in range(ROUNDS):
        set_bias(b_left, held + target_bias, feats_pad)
        part = rows.at[round_index]
        reduce_pass(b_left, a_right, part, ci, False, chunk)
        pending += exchange("col", nc, part, r_send.at[round_index], r_recv.at[round_index])
        set_bias(a_left, source_bias - merge(part[...]), feats_pad)
        part = cols.at[round_index]
        reduce_pass(a_left, b_right, part, bi, False, chunk)
        pending += exchange("blk", nb, part, c_send.at[round_index], c_recv.at[round_index])
        held = -merge(part[...])

    set_bias(b_left, held, feats_pad)
    reduce_pass(b_left, a_right, lows, ci, True, chunk)
    potential = held + target_sq
    lows[ci, gs : gs + 8, :] = jnp.broadcast_to(
        jnp.sum(target_mass * potential, axis=0, keepdims=True), (8, LANES)
    )
    pending += exchange("col", nc, lows, m_send, m_recv)
    for r in range(gs):
        lanes = slice(r * LANES, (r + 1) * LANES)
        best = jnp.max(lows[:, r, :], axis=0, keepdims=True)
        sp_ref[r : r + 1, :] = source_sq[:, lanes] - best
    target_part = jnp.sum(lows[:, gs, :], axis=0, keepdims=True)
    source_part = jnp.sum(sm_ref[...] * sp_ref[...], axis=0, keepdims=True)
    sums[bi] = jnp.broadcast_to(source_part, (8, LANES))
    pending += exchange("blk", nb, sums, d_send, d_recv)
    whole = jnp.sum(sums[...], axis=0)[0:1, :] + target_part
    db_ref[...] = jnp.sum(whole, axis=1, keepdims=True)
    cols_of = lax.broadcasted_iota(jnp.int32, potential.shape, 0)
    for g in range(gt):
        tp_ref[g : g + 1, :] = jnp.sum(
            jnp.where(cols_of == bi * gt + g, potential, 0.0), axis=0, keepdims=True
        )
    for copy in pending:
        copy.wait_send()


def local(nb, nc, source_coords, target_coords, source_mass, target_mass):
    feats, ns = source_coords.shape
    ts = target_coords.shape[1]
    nh = nb * ts
    gs, gh = ns // LANES, nh // LANES
    feats_pad = -(-feats // LANES) * LANES
    depth = feats_pad + LANES
    vmem = pl.BlockSpec(memory_space=pltpu.VMEM)
    dma = pltpu.SemaphoreType.DMA
    outs = pl.pallas_call(
        functools.partial(kernel, nb, nc, feats, feats_pad),
        out_shape=(
            jax.ShapeDtypeStruct((gs, LANES), F32),
            jax.ShapeDtypeStruct((ts // LANES, LANES), F32),
            jax.ShapeDtypeStruct((1, 1), F32),
        ),
        in_specs=[vmem] * 4,
        out_specs=(vmem,) * 3,
        scratch_shapes=[
            pltpu.VMEM((nb, feats + EXTRA, ts), F32),
            pltpu.VMEM((depth, ns), BF16),
            pltpu.VMEM((ns, depth), BF16),
            pltpu.VMEM((depth, nh), BF16),
            pltpu.VMEM((nh, depth), BF16),
            pltpu.VMEM((ROUNDS, nc, gs, LANES), F32),
            pltpu.VMEM((ROUNDS, nb, gh, LANES), F32),
            pltpu.VMEM((nc, gs + 8, LANES), F32),
            pltpu.VMEM((nb, 8, LANES), F32),
            dma((nb - 1,)), dma((nb - 1,)),
            dma((ROUNDS, nc - 1)), dma((ROUNDS, nc - 1)),
            dma((ROUNDS, nb - 1)), dma((ROUNDS, nb - 1)),
            dma((nc - 1,)), dma((nc - 1,)),
            dma((nb - 1,)), dma((nb - 1,)),
        ],
        compiler_params=pltpu.CompilerParams(
            collective_id=0, has_side_effects=True, vmem_limit_bytes=56 * 1024 * 1024
        ),
        name="transport",
    )(
        source_coords,
        target_coords,
        source_mass.reshape(gs, LANES),
        target_mass.reshape(ts // LANES, LANES),
    )
    return outs[0].reshape(ns), outs[1].reshape(ts), outs[2].reshape(())


def solution(mesh):
    in_specs = (P(None, "blk"), P(None, ("blk", "col")), P("blk"), P(("blk", "col")))
    out_specs = (P("blk"), P(("blk", "col")), P())
    body = functools.partial(local, mesh.shape["blk"], mesh.shape["col"])
    return jax.shard_map(body, mesh=mesh, in_specs=in_specs, out_specs=out_specs, check_vma=False)
```

```python
import functools

import jax
import jax.numpy as jnp
from jax import lax
from jax.experimental import pallas as pl
from jax.experimental.pallas import tpu as pltpu
from jax.sharding import PartitionSpec as P

ROUNDS = 2
EPSILON = 0.05
LANES = 128
WAYS = 4
UNROLLED = 4 * 1024
EXTRA = 8
F32 = jnp.float32
BF16 = jnp.bfloat16
SCALE = 1.4426950408889634 / EPSILON
MESH = pl.DeviceIdType.MESH


def soft(total):
    return EPSILON * jnp.log(total)


def row_tile(reds, wide):
    position = lax.broadcasted_iota(jnp.int32, (8, LANES), 0)
    out = jnp.zeros((8, LANES), F32)
    for index, part in enumerate(reds):
        out = jnp.where(position == index, jnp.broadcast_to(part, (8, LANES)), out)
    return out


def three_parts(value):
    high = value.astype(BF16).astype(F32)
    rest = value - high
    middle = rest.astype(BF16).astype(F32)
    return high, middle, rest - middle


def set_bias(left_ref, value, feats_pad):
    parts = three_parts(value)
    for r in range(value.shape[0]):
        tile = row_tile([part[r : r + 1, :] for part in parts], LANES)
        left_ref[r * LANES : (r + 1) * LANES, feats_pad : feats_pad + 8] = tile.T.astype(BF16)


def folded(values, join, ways):
    count = values.shape[0]
    step = 8
    chains = [values[w * step : (w + 1) * step, :] for w in range(ways)]
    for r in range(ways, count // step):
        chains[r % ways] = join(chains[r % ways], values[r * step : (r + 1) * step, :])
    while len(chains) > 1:
        half = len(chains) // 2
        chains = [join(chains[i], chains[i + half]) for i in range(half)]
    return chains[0]


def reduce_pass(left_ref, right_ref, out_ref, slot, hard, chunk):
    number = right_ref.shape[1] // chunk
    unrolled = number * left_ref.shape[0] <= UNROLLED

    def body(c, carry):
        lanes = pl.ds(c * chunk if unrolled else pl.multiple_of(c * chunk, chunk), chunk)
        scores = jnp.dot(left_ref[...], right_ref[:, lanes], preferred_element_type=F32)
        value = jnp.max(folded(scores, jnp.maximum, WAYS), axis=0, keepdims=True)
        if not hard:
            terms = jnp.exp2((scores - value) * SCALE)
            total = jnp.sum(folded(terms, jnp.add, WAYS), axis=0, keepdims=True)
            value = value + soft(total)
        for r in range(chunk // LANES):
            out_ref[slot, pl.ds(c * (chunk // LANES) + r, 1), :] = value[
                :, r * LANES : (r + 1) * LANES
            ]
        return carry

    if unrolled:
        for c in range(number):
            body(c, 0)
    else:
        lax.fori_loop(0, number, body, 0)


def copies(axis, extent, buf, send, recv):
    me = lax.axis_index(axis)
    started = []
    for k in range(1, extent):
        started.append(
            pltpu.make_async_remote_copy(
                src_ref=buf.at[me],
                dst_ref=buf.at[me],
                send_sem=send.at[k - 1],
                recv_sem=recv.at[k - 1],
                device_id={axis: lax.rem(me + k, extent)},
                device_id_type=MESH,
            )
        )
    return started


def arrival(axis, extent, buf, send, recv, k):
    me = lax.axis_index(axis)
    origin = lax.rem(me + extent - k, extent)
    return pltpu.make_async_remote_copy(
        src_ref=buf.at[origin],
        dst_ref=buf.at[origin],
        send_sem=send.at[k - 1],
        recv_sem=recv.at[k - 1],
        device_id={axis: origin},
        device_id_type=MESH,
    )


def exchange(axis, extent, buf, send, recv):
    started = copies(axis, extent, buf, send, recv)
    for copy in started:
        copy.start()
    for k in range(1, extent):
        arrival(axis, extent, buf, send, recv, k).wait_recv()
    return started


def merge(parts):
    top = jnp.max(parts, axis=0)
    return top + soft(jnp.sum(jnp.exp2((parts - top[None]) * SCALE), axis=0))


def kernel(
    nb, nc, feats, feats_pad,
    sc_any, tc_any, sm_any, tm_any,
    sp_ref, tp_ref, db_ref,
    sc_ref, tc_ref, sm_ref, tm_ref, in_sem, f_send, f_recv, blocks, a_right, a_left, b_right, b_left, rows, cols, lows, sums,
    g_send, g_recv, r_send, r_recv, c_send, c_recv, m_send, m_recv, d_send, d_recv,
):
    bi = lax.axis_index("blk")
    ci = lax.axis_index("col")
    ns = sc_ref.shape[1]
    ts = tc_ref.shape[1]
    gs = ns // LANES
    gt = ts // LANES
    loads = [
        pltpu.make_async_copy(src, dst, in_sem.at[index])
        for index, (src, dst) in enumerate(
            ((tc_any, tc_ref), (tm_any, tm_ref), (sc_any, sc_ref), (sm_any, sm_ref))
        )
    ]
    for load in loads:
        load.start()
    barrier = pltpu.get_barrier_semaphore()
    for k in range(1, nb):
        pl.semaphore_signal(barrier, inc=1, device_id={"blk": lax.rem(bi + k, nb)}, device_id_type=MESH)
    for k in range(1, nc):
        pl.semaphore_signal(barrier, inc=1, device_id={"col": lax.rem(ci + k, nc)}, device_id_type=MESH)

    loads[0].wait()
    loads[1].wait()
    own = tc_ref[...].astype(F32)
    blocks[bi, 0:feats, :] = own
    for g in range(gt):
        lanes = slice(g * LANES, (g + 1) * LANES)
        blocks[bi, feats : feats + EXTRA, lanes] = row_tile(
            [tm_ref[g : g + 1, :], jnp.sum(jnp.square(own[:, lanes]), axis=0, keepdims=True)], LANES
        )

    depth = a_right.shape[0]
    ones = lambda width: jnp.where(
        lax.broadcasted_iota(jnp.int32, (depth - feats_pad, width), 0) < 3, 1.0, 0.0
    ).astype(BF16)

    half = nb // 2
    sibling = bi + 1 - 2 * lax.rem(bi, 2)

    def shipment(block, peer, send, recv):
        return pltpu.make_async_remote_copy(
            src_ref=blocks.at[block],
            dst_ref=blocks.at[block],
            send_sem=send,
            recv_sem=recv,
            device_id={"blk": peer},
            device_id_type=MESH,
        )

    pl.semaphore_wait(barrier, nb + nc - 2)
    gathers = [
        shipment(bi, lax.rem(bi + 2 * j, nb), g_send.at[j], g_recv.at[j]) for j in range(1, half)
    ]
    gathers.append(shipment(bi, sibling, g_send.at[0], g_recv.at[0]))
    for copy in gathers:
        copy.start()
    loads[2].wait()
    loads[3].wait()

    a_right[0:feats, :] = sc_ref[...]
    if feats_pad > feats:
        a_right[feats:feats_pad, :] = jnp.zeros((feats_pad - feats, ns), BF16)
        b_right[feats:feats_pad, :] = jnp.zeros((feats_pad - feats, b_right.shape[1]), BF16)
    a_right[feats_pad:depth, :] = ones(ns)
    b_right[feats_pad:depth, :] = ones(b_right.shape[1])
    wide = sc_ref[...].astype(F32)
    source_sq = jnp.sum(jnp.square(wide), axis=0, keepdims=True)
    for r in range(gs):
        rows_of = slice(r * LANES, (r + 1) * LANES)
        piece = jnp.concatenate(
            [wide[:, rows_of], jnp.zeros((feats_pad - feats, LANES), F32)], axis=0
        )
        a_left[rows_of, 0:feats_pad] = piece.T.astype(BF16)
    a_left[:, feats_pad:depth] = jnp.zeros((ns, depth - feats_pad), BF16)
    b_left[:, feats_pad:depth] = jnp.zeros((b_left.shape[0], depth - feats_pad), BF16)
    source_bias = EPSILON * jnp.log(sm_ref[...])

    def unpack(b):
        for g in range(gt):
            lanes = slice(g * LANES, (g + 1) * LANES)
            rows_of = pl.ds(pl.multiple_of(b * ts + g * LANES, LANES), LANES)
            piece = 2.0 * blocks[b, 0:feats, lanes]
            b_right[0:feats, rows_of] = piece.astype(BF16)
            if feats_pad > feats:
                piece = jnp.concatenate(
                    [piece, jnp.zeros((feats_pad - feats, LANES), F32)], axis=0
                )
            b_left[rows_of, 0:feats_pad] = piece.T.astype(BF16)

    unpack(bi)
    shipment(sibling, sibling, g_send.at[0], g_recv.at[0]).wait_recv()
    unpack(sibling)
    order = [j // 2 + 1 if j % 2 == 0 else half - 1 - j // 2 for j in range(half - 1)]
    for j in order:
        origin = lax.rem(bi + nb - 2 * j, nb)
        shipment(origin, origin, g_send.at[j], g_recv.at[j]).wait_recv()
        forward = shipment(origin, sibling, f_send.at[j], f_recv.at[j])
        forward.start()
        gathers.append(forward)
        unpack(origin)
    for j in order:
        origin = lax.rem(sibling + nb - 2 * j, nb)
        shipment(origin, sibling, f_send.at[j], f_recv.at[j]).wait_recv()
        unpack(origin)
    masses = []
    squares = []
    for b in range(nb):
        for g in range(gt):
            lanes = slice(g * LANES, (g + 1) * LANES)
            masses.append(blocks[b, feats : feats + 1, lanes])
            squares.append(blocks[b, feats + 1 : feats + 2, lanes])
    target_mass = jnp.concatenate(masses, axis=0)
    target_sq = jnp.concatenate(squares, axis=0)
    target_bias = EPSILON * jnp.log(target_mass)

    chunk = 256
    pending = list(gathers)
    held = -target_sq
    for round_index in range(ROUNDS):
        set_bias(b_left, held + target_bias, feats_pad)
        part = rows.at[round_index]
        reduce_pass(b_left, a_right, part, ci, False, chunk)
        pending += exchange("col", nc, part, r_send.at[round_index], r_recv.at[round_index])
        set_bias(a_left, source_bias - merge(part[...]), feats_pad)
        part = cols.at[round_index]
        reduce_pass(a_left, b_right, part, bi, False, chunk)
        pending += exchange("blk", nb, part, c_send.at[round_index], c_recv.at[round_index])
        held = -merge(part[...])

    set_bias(b_left, held, feats_pad)
    reduce_pass(b_left, a_right, lows, ci, True, chunk)
    potential = held + target_sq
    lows[ci, gs : gs + 8, :] = jnp.broadcast_to(
        jnp.sum(target_mass * potential, axis=0, keepdims=True), (8, LANES)
    )
    cols_of = lax.broadcasted_iota(jnp.int32, potential.shape, 0)
    for g in range(gt):
        tp_ref[g : g + 1, :] = jnp.sum(
            jnp.where(cols_of == bi * gt + g, potential, 0.0), axis=0, keepdims=True
        )
    pending += exchange("col", nc, lows, m_send, m_recv)
    for r in range(gs):
        lanes = slice(r * LANES, (r + 1) * LANES)
        best = jnp.max(lows[:, r, :], axis=0, keepdims=True)
        sp_ref[r : r + 1, :] = source_sq[:, lanes] - best
    target_part = jnp.sum(lows[:, gs, :], axis=0, keepdims=True)
    source_part = jnp.sum(sm_ref[...] * sp_ref[...], axis=0, keepdims=True)
    sums[bi] = jnp.broadcast_to(source_part, (8, LANES))
    pending += exchange("blk", nb, sums, d_send, d_recv)
    whole = jnp.sum(sums[...], axis=0)[0:1, :] + target_part
    db_ref[...] = jnp.sum(whole, axis=1, keepdims=True)
    for copy in pending:
        copy.wait_send()


def local(nb, nc, source_coords, target_coords, source_mass, target_mass):
    feats, ns = source_coords.shape
    ts = target_coords.shape[1]
    nh = nb * ts
    gs, gh = ns // LANES, nh // LANES
    feats_pad = -(-feats // LANES) * LANES
    depth = feats_pad + LANES
    vmem = pl.BlockSpec(memory_space=pltpu.VMEM)
    dma = pltpu.SemaphoreType.DMA
    outs = pl.pallas_call(
        functools.partial(kernel, nb, nc, feats, feats_pad),
        out_shape=(
            jax.ShapeDtypeStruct((gs, LANES), F32),
            jax.ShapeDtypeStruct((ts // LANES, LANES), F32),
            jax.ShapeDtypeStruct((1, 1), F32),
        ),
        in_specs=[pl.BlockSpec(memory_space=pl.ANY)] * 4,
        out_specs=(vmem,) * 3,
        scratch_shapes=[
            pltpu.VMEM((feats, ns), BF16),
            pltpu.VMEM((feats, ts), BF16),
            pltpu.VMEM((gs, LANES), F32),
            pltpu.VMEM((ts // LANES, LANES), F32),
            dma((4,)), dma((nb // 2,)), dma((nb // 2,)),
            pltpu.VMEM((nb, feats + EXTRA, ts), F32),
            pltpu.VMEM((depth, ns), BF16),
            pltpu.VMEM((ns, depth), BF16),
            pltpu.VMEM((depth, nh), BF16),
            pltpu.VMEM((nh, depth), BF16),
            pltpu.VMEM((ROUNDS, nc, gs, LANES), F32),
            pltpu.VMEM((ROUNDS, nb, gh, LANES), F32),
            pltpu.VMEM((nc, gs + 8, LANES), F32),
            pltpu.VMEM((nb, 8, LANES), F32),
            dma((nb // 2,)), dma((nb // 2,)),
            dma((ROUNDS, nc - 1)), dma((ROUNDS, nc - 1)),
            dma((ROUNDS, nb - 1)), dma((ROUNDS, nb - 1)),
            dma((nc - 1,)), dma((nc - 1,)),
            dma((nb - 1,)), dma((nb - 1,)),
        ],
        compiler_params=pltpu.CompilerParams(
            collective_id=0, has_side_effects=True, vmem_limit_bytes=56 * 1024 * 1024
        ),
        name="transport",
    )(
        source_coords,
        target_coords,
        source_mass.reshape(gs, LANES),
        target_mass.reshape(ts // LANES, LANES),
    )
    return outs[0].reshape(ns), outs[1].reshape(ts), outs[2].reshape(())


def solution(mesh):
    in_specs = (P(None, "blk"), P(None, ("blk", "col")), P("blk"), P(("blk", "col")))
    out_specs = (P("blk"), P(("blk", "col")), P())
    body = functools.partial(local, mesh.shape["blk"], mesh.shape["col"])
    return jax.shard_map(body, mesh=mesh, in_specs=in_specs, out_specs=out_specs, check_vma=False)
```

```python
import functools

import jax
import jax.numpy as jnp
from jax import lax
from jax.experimental import pallas as pl
from jax.experimental.pallas import tpu as pltpu
from jax.sharding import PartitionSpec as P

ROUNDS = 2
EPSILON = 0.05
LANES = 128
WAYS = 8
UNROLLED = 4 * 1024
EXTRA = 8
F32 = jnp.float32
BF16 = jnp.bfloat16
SCALE = 1.4426950408889634 / EPSILON
MESH = pl.DeviceIdType.MESH


def soft(total):
    return EPSILON * jnp.log(total)


def row_tile(reds, wide):
    position = lax.broadcasted_iota(jnp.int32, (8, LANES), 0)
    out = jnp.zeros((8, LANES), F32)
    for index, part in enumerate(reds):
        out = jnp.where(position == index, jnp.broadcast_to(part, (8, LANES)), out)
    return out


def three_parts(value):
    high = value.astype(BF16).astype(F32)
    rest = value - high
    middle = rest.astype(BF16).astype(F32)
    return high, middle, rest - middle


def set_bias(left_ref, value, feats_pad):
    parts = three_parts(value)
    for r in range(value.shape[0]):
        tile = row_tile([part[r : r + 1, :] for part in parts], LANES)
        left_ref[r * LANES : (r + 1) * LANES, feats_pad : feats_pad + 8] = tile.T.astype(BF16)


def folded(values, join, ways):
    count = values.shape[0]
    step = 8
    chains = [values[w * step : (w + 1) * step, :] for w in range(ways)]
    for r in range(ways, count // step):
        chains[r % ways] = join(chains[r % ways], values[r * step : (r + 1) * step, :])
    while len(chains) > 1:
        half = len(chains) // 2
        chains = [join(chains[i], chains[i + half]) for i in range(half)]
    return chains[0]


def reduce_pass(left_ref, right_ref, out_ref, slot, hard, chunk):
    number = right_ref.shape[1] // chunk
    unrolled = number * left_ref.shape[0] <= UNROLLED

    def body(c, carry):
        lanes = pl.ds(c * chunk if unrolled else pl.multiple_of(c * chunk, chunk), chunk)
        scores = jnp.dot(left_ref[...], right_ref[:, lanes], preferred_element_type=F32)
        value = jnp.max(folded(scores, jnp.maximum, WAYS), axis=0, keepdims=True)
        if not hard:
            terms = jnp.exp2((scores - value) * SCALE)
            total = jnp.sum(folded(terms, jnp.add, WAYS), axis=0, keepdims=True)
            value = value + soft(total)
        for r in range(chunk // LANES):
            out_ref[slot, pl.ds(c * (chunk // LANES) + r, 1), :] = value[
                :, r * LANES : (r + 1) * LANES
            ]
        return carry

    if unrolled:
        for c in range(number):
            body(c, 0)
    else:
        lax.fori_loop(0, number, body, 0)


def copies(axis, extent, buf, send, recv):
    me = lax.axis_index(axis)
    started = []
    for k in range(1, extent):
        started.append(
            pltpu.make_async_remote_copy(
                src_ref=buf.at[me],
                dst_ref=buf.at[me],
                send_sem=send.at[k - 1],
                recv_sem=recv.at[k - 1],
                device_id={axis: lax.rem(me + k, extent)},
                device_id_type=MESH,
            )
        )
    return started


def arrival(axis, extent, buf, send, recv, k):
    me = lax.axis_index(axis)
    origin = lax.rem(me + extent - k, extent)
    return pltpu.make_async_remote_copy(
        src_ref=buf.at[origin],
        dst_ref=buf.at[origin],
        send_sem=send.at[k - 1],
        recv_sem=recv.at[k - 1],
        device_id={axis: origin},
        device_id_type=MESH,
    )


def exchange(axis, extent, buf, send, recv):
    started = copies(axis, extent, buf, send, recv)
    for copy in started:
        copy.start()
    for k in range(1, extent):
        arrival(axis, extent, buf, send, recv, k).wait_recv()
    return started


def merge(parts):
    top = jnp.max(parts, axis=0)
    return top + soft(jnp.sum(jnp.exp2((parts - top[None]) * SCALE), axis=0))


def kernel(
    nb, nc, feats, feats_pad,
    sc_any, tc_any, sm_any, tm_any,
    sp_ref, tp_ref, db_ref,
    sc_ref, tc_ref, sm_ref, tm_ref, in_sem, f_send, f_recv, firsts, blocks, a_right, a_left, b_right, b_left, rows, cols, lows, sums,
    g_send, g_recv, r_send, r_recv, c_send, c_recv, m_send, m_recv, d_send, d_recv,
):
    bi = lax.axis_index("blk")
    ci = lax.axis_index("col")
    ns = sc_ref.shape[1]
    ts = tc_ref.shape[1]
    gs = ns // LANES
    gt = ts // LANES
    loads = [
        pltpu.make_async_copy(src, dst, in_sem.at[index])
        for index, (src, dst) in enumerate(
            ((tc_any, tc_ref), (tm_any, tm_ref), (sc_any, sc_ref), (sm_any, sm_ref))
        )
    ]
    for load in loads:
        load.start()
    barrier = pltpu.get_barrier_semaphore()
    for k in range(1, nb):
        pl.semaphore_signal(barrier, inc=1, device_id={"blk": lax.rem(bi + k, nb)}, device_id_type=MESH)
    for k in range(1, nc):
        pl.semaphore_signal(barrier, inc=1, device_id={"col": lax.rem(ci + k, nc)}, device_id_type=MESH)

    loads[0].wait()
    loads[1].wait()
    own = tc_ref[...].astype(F32)
    blocks[bi, 0:feats, :] = own
    for g in range(gt):
        lanes = slice(g * LANES, (g + 1) * LANES)
        blocks[bi, feats : feats + EXTRA, lanes] = row_tile(
            [tm_ref[g : g + 1, :], jnp.sum(jnp.square(own[:, lanes]), axis=0, keepdims=True)], LANES
        )

    depth = a_right.shape[0]
    ones = lambda width: jnp.where(
        lax.broadcasted_iota(jnp.int32, (depth - feats_pad, width), 0) < 3, 1.0, 0.0
    ).astype(BF16)

    half = nb // 2
    sibling = bi + 1 - 2 * lax.rem(bi, 2)

    def shipment(block, peer, send, recv):
        return pltpu.make_async_remote_copy(
            src_ref=blocks.at[block],
            dst_ref=blocks.at[block],
            send_sem=send,
            recv_sem=recv,
            device_id={"blk": peer},
            device_id_type=MESH,
        )

    pl.semaphore_wait(barrier, nb + nc - 2)
    gathers = [
        shipment(bi, lax.rem(bi + 2 * j, nb), g_send.at[j], g_recv.at[j]) for j in range(1, half)
    ]
    gathers.append(shipment(bi, sibling, g_send.at[0], g_recv.at[0]))
    for copy in gathers:
        copy.start()
    loads[2].wait()
    loads[3].wait()

    a_right[0:feats, :] = sc_ref[...]
    if feats_pad > feats:
        a_right[feats:feats_pad, :] = jnp.zeros((feats_pad - feats, ns), BF16)
        b_right[feats:feats_pad, :] = jnp.zeros((feats_pad - feats, b_right.shape[1]), BF16)
    a_right[feats_pad:depth, :] = ones(ns)
    b_right[feats_pad:depth, :] = ones(b_right.shape[1])
    wide = sc_ref[...].astype(F32)
    source_sq = jnp.sum(jnp.square(wide), axis=0, keepdims=True)
    b_left[:, feats_pad:depth] = jnp.zeros((b_left.shape[0], depth - feats_pad), BF16)
    source_bias = EPSILON * jnp.log(sm_ref[...])

    def unpack(b):
        for g in range(gt):
            lanes = slice(g * LANES, (g + 1) * LANES)
            rows_of = pl.ds(pl.multiple_of(b * ts + g * LANES, LANES), LANES)
            piece = 2.0 * blocks[b, 0:feats, lanes]
            b_right[0:feats, rows_of] = piece.astype(BF16)
            if feats_pad > feats:
                piece = jnp.concatenate(
                    [piece, jnp.zeros((feats_pad - feats, LANES), F32)], axis=0
                )
            b_left[rows_of, 0:feats_pad] = piece.T.astype(BF16)
            bias = EPSILON * jnp.log(blocks[b, feats : feats + 1, lanes])
            set_bias(
                b_left.at[rows_of, :], bias - blocks[b, feats + 1 : feats + 2, lanes], feats_pad
            )

    unpack(bi)
    for r in range(gs):
        rows_of = slice(r * LANES, (r + 1) * LANES)
        piece = jnp.concatenate(
            [wide[:, rows_of], jnp.zeros((feats_pad - feats, LANES), F32)], axis=0
        )
        a_left[rows_of, 0:feats_pad] = piece.T.astype(BF16)
    a_left[:, feats_pad:depth] = jnp.zeros((ns, depth - feats_pad), BF16)
    shipment(sibling, sibling, g_send.at[0], g_recv.at[0]).wait_recv()
    unpack(sibling)
    order = [j // 2 + 1 if j % 2 == 0 else half - 1 - j // 2 for j in range(half - 1)]
    def relay(j):
        origin = lax.rem(bi + nb - 2 * j, nb)
        shipment(origin, origin, g_send.at[j], g_recv.at[j]).wait_recv()
        forward = shipment(origin, sibling, f_send.at[j], f_recv.at[j])
        forward.start()
        gathers.append(forward)
        return origin

    def relayed(j):
        origin = lax.rem(sibling + nb - 2 * j, nb)
        shipment(origin, sibling, f_send.at[j], f_recv.at[j]).wait_recv()
        unpack(origin)

    for index, j in enumerate(order):
        if index >= 2:
            relayed(order[index - 2])
        origin = relay(j)
        if index + 1 < len(order):
            unpack(origin)
        else:
            if index >= 1:
                relayed(order[index - 1])
            unpack(origin)
            relayed(j)
    masses = []
    squares = []
    for b in range(nb):
        for g in range(gt):
            lanes = slice(g * LANES, (g + 1) * LANES)
            masses.append(blocks[b, feats : feats + 1, lanes])
            squares.append(blocks[b, feats + 1 : feats + 2, lanes])
    target_mass = jnp.concatenate(masses, axis=0)
    target_sq = jnp.concatenate(squares, axis=0)
    target_bias = EPSILON * jnp.log(target_mass)

    chunk = 256
    pending = list(gathers)
    held = None
    for round_index in range(ROUNDS):
        part = rows.at[round_index]
        if round_index == 0:
            reduce_pass(b_left, a_right, part, ci, False, chunk)
        else:
            set_bias(b_left, held + target_bias, feats_pad)
            reduce_pass(b_left, a_right, part, ci, False, chunk)
        pending += exchange("col", nc, part, r_send.at[round_index], r_recv.at[round_index])
        set_bias(a_left, source_bias - merge(part[...]), feats_pad)
        part = cols.at[round_index]
        reduce_pass(a_left, b_right, part, bi, False, chunk)
        pending += exchange("blk", nb, part, c_send.at[round_index], c_recv.at[round_index])
        held = -merge(part[...])

    set_bias(b_left, held, feats_pad)
    reduce_pass(b_left, a_right, lows, ci, True, chunk)
    potential = held + target_sq
    lows[ci, gs : gs + 8, :] = jnp.broadcast_to(
        jnp.sum(target_mass * potential, axis=0, keepdims=True), (8, LANES)
    )
    cols_of = lax.broadcasted_iota(jnp.int32, potential.shape, 0)
    for g in range(gt):
        tp_ref[g : g + 1, :] = jnp.sum(
            jnp.where(cols_of == bi * gt + g, potential, 0.0), axis=0, keepdims=True
        )
    pending += exchange("col", nc, lows, m_send, m_recv)
    for r in range(gs):
        lanes = slice(r * LANES, (r + 1) * LANES)
        best = jnp.max(lows[:, r, :], axis=0, keepdims=True)
        sp_ref[r : r + 1, :] = source_sq[:, lanes] - best
    target_part = jnp.sum(lows[:, gs, :], axis=0, keepdims=True)
    source_part = jnp.sum(sm_ref[...] * sp_ref[...], axis=0, keepdims=True)
    sums[bi] = jnp.broadcast_to(source_part, (8, LANES))
    pending += exchange("blk", nb, sums, d_send, d_recv)
    whole = jnp.sum(sums[...], axis=0)[0:1, :] + target_part
    db_ref[...] = jnp.sum(whole, axis=1, keepdims=True)
    for copy in pending:
        copy.wait_send()


def local(nb, nc, source_coords, target_coords, source_mass, target_mass):
    feats, ns = source_coords.shape
    ts = target_coords.shape[1]
    nh = nb * ts
    gs, gh = ns // LANES, nh // LANES
    feats_pad = -(-feats // LANES) * LANES
    depth = feats_pad + LANES
    vmem = pl.BlockSpec(memory_space=pltpu.VMEM)
    dma = pltpu.SemaphoreType.DMA
    outs = pl.pallas_call(
        functools.partial(kernel, nb, nc, feats, feats_pad),
        out_shape=(
            jax.ShapeDtypeStruct((gs, LANES), F32),
            jax.ShapeDtypeStruct((ts // LANES, LANES), F32),
            jax.ShapeDtypeStruct((1, 1), F32),
        ),
        in_specs=[pl.BlockSpec(memory_space=pl.ANY)] * 4,
        out_specs=(vmem,) * 3,
        scratch_shapes=[
            pltpu.VMEM((feats, ns), BF16),
            pltpu.VMEM((feats, ts), BF16),
            pltpu.VMEM((gs, LANES), F32),
            pltpu.VMEM((ts // LANES, LANES), F32),
            dma((4,)), dma((nb // 2,)), dma((nb // 2,)),
            pltpu.VMEM((nb, gs, LANES), F32),
            pltpu.VMEM((nb, feats + EXTRA, ts), F32),
            pltpu.VMEM((depth, ns), BF16),
            pltpu.VMEM((ns, depth), BF16),
            pltpu.VMEM((depth, nh), BF16),
            pltpu.VMEM((nh, depth), BF16),
            pltpu.VMEM((ROUNDS, nc, gs, LANES), F32),
            pltpu.VMEM((ROUNDS, nb, gh, LANES), F32),
            pltpu.VMEM((nc, gs + 8, LANES), F32),
            pltpu.VMEM((nb, 8, LANES), F32),
            dma((nb // 2,)), dma((nb // 2,)),
            dma((ROUNDS, nc - 1)), dma((ROUNDS, nc - 1)),
            dma((ROUNDS, nb - 1)), dma((ROUNDS, nb - 1)),
            dma((nc - 1,)), dma((nc - 1,)),
            dma((nb - 1,)), dma((nb - 1,)),
        ],
        compiler_params=pltpu.CompilerParams(
            collective_id=0, has_side_effects=True, vmem_limit_bytes=56 * 1024 * 1024
        ),
        name="transport",
    )(
        source_coords,
        target_coords,
        source_mass.reshape(gs, LANES),
        target_mass.reshape(ts // LANES, LANES),
    )
    return outs[0].reshape(ns), outs[1].reshape(ts), outs[2].reshape(())


def solution(mesh):
    in_specs = (P(None, "blk"), P(None, ("blk", "col")), P("blk"), P(("blk", "col")))
    out_specs = (P("blk"), P(("blk", "col")), P())
    body = functools.partial(local, mesh.shape["blk"], mesh.shape["col"])
    return jax.shard_map(body, mesh=mesh, in_specs=in_specs, out_specs=out_specs, check_vma=False)
```
